512 devices in a mesh: occ: 8 (over x_lo, y), aux: 64 (over z, x_hi, core).
Axes of the slice: x: 4 (x_hi: 2, x_lo: 2; x = x_hi * 2 + x_lo), y: 4, z: 16, core: 2. Of those that a mesh axis runs over, the one named last changes fastest.
Arguments:
- factors: float32 [8, 640, 24576], P('occ', None, 'aux'), may hold values from -1.75 to 1.75
- occ_energy: float32 [32], replicated, may hold values from -1.5 to -0.3
- vir_energy: float32 [640], replicated, may hold values from 0.2 to 4
- orbital: int32 [8], replicated, may hold values from 0 to 31
- vir_index: int32 [640], replicated, may hold values from 0 to 639, each once
Outputs:
- density: float32 [8, 640, 24576], P('occ', None, 'aux')
The draws below stay inside these ranges and needn't reach their ends.
Inputs may be any that keep to these rules, and one draw needn't show every extreme that they name: `vir_index`: each virtual's row appears once.
All inputs are finite; a program needn't handle non-finite values.
Results may differ from the reference program's by a relative error of at most 0.0001.
Values sent between devices are 32-bit elements; how exact they have to be, the bound alone decides.
No kernel may reach another device: no remote copies, remote signals or barrier semaphores. Data moves between devices by JAX's collectives and lax.ppermute only.
A program may use at most 64 MiB of HBM per device.

```python
import jax
import jax.numpy as jnp
from jax import lax

V = 640
NAUX = 24576
ORBS = 8
OCC_ALL = 32
N_OCC = 8


def place_ends(entries, rng, low, top_value):
    extent = entries.shape
    spot = [jax.random.randint(jax.random.fold_in(rng, axis), (), 0, extent[axis]) for axis in range(len(extent))]
    entries = entries.at[tuple(spot)].set(low)
    longest = extent.index(max(extent))
    spot[longest] = (spot[longest] + 1) % extent[longest]
    return entries.at[tuple(spot)].set(top_value)


def spiked(array, key, source, target, parts, factor):
    def block_of(position):
        return (jnp.arange(array.shape[position]) // (array.shape[position] // parts)).reshape((-1,) + (1,) * (array.ndim - 1 - position))

    one_side = jax.random.permutation(key, parts)[block_of(target)]
    far = (block_of(target) + parts // 2) % parts
    return jnp.where((block_of(source) == one_side) | (block_of(source) == far), factor * array, array)


def block_scale(stream_key, shape, cuts, smallest, top_value):
    gain, own = 1.0, jax.random.fold_in(stream_key, 6)
    for dim, parts in cuts:
        heights = jnp.exp(jax.random.uniform(jax.random.fold_in(own, dim), (parts,), jnp.float32, smallest / len(cuts), top_value / len(cuts)))
        gain = gain * jnp.repeat(heights, shape[dim] // parts).reshape([-1 if axis == dim else 1 for axis in range(len(shape))])
    return gain


def noise_with(rng, extent, deviation, limit, pieces, heavy, held_as=jnp.bfloat16):
    result = deviation * jax.random.normal(rng, extent, jnp.float32)
    if pieces:
        result = result * block_scale(rng, extent, pieces, -0.22, 0.18)
    return jnp.clip(spiked(result, jax.random.fold_in(rng, 3), *heavy), -limit, limit).astype(held_as)


def setup_inputs(seed: int = 0) -> dict:
    arg_keys = jax.random.split(jax.random.key(seed), 6)
    factors = noise_with(arg_keys[0], (ORBS, V, NAUX), 0.1, 1.75, ((0, 8), (2, 64)), (2, 1, 64, 4.0), jnp.float32)
    occ_energy = jnp.clip(jax.random.uniform(arg_keys[1], (OCC_ALL,), jnp.float32, -1.5, -0.3), -1.5, -0.3)
    vir_energy = jnp.clip(jax.random.uniform(arg_keys[2], (V,), jnp.float32, 0.2, 4.0), 0.2, 4.0)
    orbital = place_ends(jax.random.randint(arg_keys[3], (ORBS,), 0, OCC_ALL), jax.random.fold_in(arg_keys[3], 1), 0, OCC_ALL - 1).astype(jnp.int32)
    vir_index = jax.random.permutation(arg_keys[4], V).astype(jnp.int32)
    return dict(factors=factors, occ_energy=occ_energy, vir_energy=vir_energy, orbital=orbital, vir_index=vir_index)


highest = lax.Precision.HIGHEST


def reference(factors, occ_energy, vir_energy, orbital, vir_index):
    virtual_energy = vir_energy[vir_index]
    orbital_energy = occ_energy[orbital]
    totals = [jnp.zeros((V, NAUX), jnp.float32) for _ in range(N_OCC)]
    for first in range(N_OCC):
        for offset in (1, 3):
            second = (first + offset) % N_OCC
            integrals = lax.dot_general(factors[first], factors[second], (((1,), (1,)), ((), ())), precision=highest, preferred_element_type=jnp.float32)
            denominator = orbital_energy[first] + orbital_energy[second] - virtual_energy[:, None] - virtual_energy[None, :]
            amplitude = integrals / denominator
            totals[first] = totals[first] + jnp.dot(amplitude, factors[second], precision=highest, preferred_element_type=jnp.float32)
            totals[second] = totals[second] + lax.dot_general(amplitude, factors[first], (((0,), (0,)), ((), ())), precision=highest, preferred_element_type=jnp.float32)
    return jnp.stack(totals)
```

```python
import jax
import jax.numpy as jnp
from jax import lax
from jax.sharding import PartitionSpec as P

XL, Y, Z, XH, CORE = 2, 4, 16, 2, 2
RING = Z // 2

STEPS = (
    (1, 0, 3, 2, 5, 4, 7, 6),
    (7, 2, 1, 4, 3, 6, 5, 0),
    (3, 6, 5, 0, 7, 2, 1, 4),
)
KEEPS = (
    (0, 1, 1, 0, 0, 1, 1, 0),
    (0, 0, 1, 0, 1, 1, 0, 1),
)


def flat(place):
    xl, y, z, xh, core = place
    return (((xl * Y + y) * Z + z) * XH + xh) * CORE + core


def places():
    return [
        (xl, y, z, xh, core)
        for xl in range(XL)
        for y in range(Y)
        for z in range(Z)
        for xh in range(XH)
        for core in range(CORE)
    ]


def partner_z(z, core):
    return z ^ 1 if core == 0 else ((z - 1) ^ 1) + 1 & 15


def partner_xy(xl, y, z):
    return (xl, (y + 1) % Y) if z % 2 == 0 else (1 - xl, (y - 1) % Y)


def beside(place):
    xl, y, z, xh, core = place
    return (xl, y, partner_z(z, core), xh, core)


def across(place):
    xl, y, z, xh, core = place
    return (*partner_xy(xl, y, z), z, xh, core)


def diagonal(place):
    xl, y, z, xh, core = place
    return (*partner_xy(xl, y, z), partner_z(z, core), xh, core)


def other_core(place):
    return (*place[:4], 1 - place[4])


def other_half(place):
    xl, y, z, xh, core = place
    return (xl, y, z, 1 - xh, core)


def ring_partner(stage):
    def partner(place):
        xl, y, z, xh, core = place
        r, parity = z // 2, z % 2
        if core == 0:
            r = STEPS[stage][r]
        else:
            r = -STEPS[stage][-r % RING] % RING
        return (xl, y, 2 * r + parity, xh, core)

    return partner


def fetch(value, source_of):
    return lax.ppermute(value, ("occ", "aux"), [(flat(source_of(p)), flat(p)) for p in places()])


def deliver(value, target_of):
    return lax.ppermute(value, ("occ", "aux"), [(flat(p), flat(target_of(p))) for p in places()])


def dot(left, right, dims):
    return lax.dot_general(left, right, (dims, ((), ())), precision=lax.Precision.HIGH, preferred_element_type=jnp.float32)


def table_pick(table, indices):
    matches = indices[:, None] == jnp.arange(table.shape[0], dtype=jnp.int32)[None, :]
    return jnp.sum(jnp.where(matches, table[None, :], 0.0), axis=1)


def scalar_pick(values, position):
    matches = jnp.arange(values.shape[0], dtype=jnp.int32) == position
    return jnp.sum(jnp.where(matches, values, jnp.zeros_like(values)))


def scattered(value, upper, partner):
    half = value.shape[0] // 2
    low, high = value[:half], value[half:]
    received = fetch(jnp.where(upper, low, high), partner)
    return jnp.where(upper, high, low) + received


def gathered(value, upper, partner):
    received = fetch(value, partner)
    return jnp.concatenate([jnp.where(upper, received, value), jnp.where(upper, value, received)], axis=0)


def body(factors, occ_energy, vir_energy, orbital, vir_index):
    mine = factors[0]
    occ, aux = lax.axis_index("occ"), lax.axis_index("aux")
    core, xh, z = aux % 2, aux // 2 % 2, aux // 4
    xl, y = occ // Y, occ % Y
    near = z % 2 == 0
    partner = jnp.where(near, xl * Y + (y + 1) % Y, (1 - xl) * Y + (y + 3) % Y)
    ring = jnp.where(core == 0, z // 2, -(z // 2) % RING)
    keeps = [scalar_pick(jnp.array(k, jnp.int32), ring) for k in KEEPS]
    halves = [core == 1, xh == 1, keeps[0] == 1, keeps[1] == 1]
    partners = [other_core, other_half, ring_partner(0), ring_partner(1)]

    theirs = fetch(mine, across)
    mine_beside = fetch(mine, beside)
    theirs_beside = fetch(mine, diagonal)

    integrals = dot(mine, theirs, ((1,), (1,))) + dot(mine_beside, theirs_beside, ((1,), (1,)))
    for upper, partner_of in zip(halves, partners):
        integrals = scattered(integrals, upper, partner_of)
    integrals = integrals + fetch(integrals, ring_partner(2))

    rows = integrals.shape[0]
    start = core * 320 + xh * 160 + keeps[0] * 80 + keeps[1] * 40
    virtual = table_pick(vir_energy, vir_index)
    virtual_rows = table_pick(vir_energy, lax.dynamic_slice(vir_index, (start,), (rows,)))
    energy = table_pick(occ_energy, orbital)
    pair_energy = scalar_pick(energy, occ) + scalar_pick(energy, partner)
    amplitude = integrals / (pair_energy - virtual_rows[:, None] - virtual[None, :])

    for upper, partner_of in zip(halves[::-1], partners[::-1]):
        amplitude = gathered(amplitude, upper, partner_of)

    from_diagonal = deliver(dot(amplitude, mine_beside, ((0,), (0,))), diagonal)
    from_across = deliver(dot(amplitude, mine, ((0,), (0,))), across)
    from_beside = deliver(dot(amplitude, theirs_beside, ((1,), (0,))), beside)
    total = dot(amplitude, theirs, ((1,), (0,))) + from_beside + from_across + from_diagonal
    return total[None]


def solution(mesh):
    return jax.shard_map(
        body,
        mesh=mesh,
        in_specs=(P("occ", None, "aux"), P(), P(), P(), P()),
        out_specs=P("occ", None, "aux"),
        check_vma=False,
    )
```

```python
import jax
import jax.numpy as jnp
from jax import lax
from jax.sharding import PartitionSpec as P


XL, Y, Z, XH, CORE = 2, 4, 16, 2, 2
SPLITS = (256, 384)
JUMPS = (1, -1, 3, -5)


def flat(place):
    xl, y, z, xh, core = place
    return (((xl * Y + y) * Z + z) * XH + xh) * CORE + core


def places():
    return [
        (xl, y, z, xh, core)
        for xl in range(XL)
        for y in range(Y)
        for z in range(Z)
        for xh in range(XH)
        for core in range(CORE)
    ]


def pair_partner(place):
    xl, y, z, xh, core = place
    return (xl, (y + 1) % Y, z, xh, core) if core == 0 else (1 - xl, (y - 1) % Y, z, xh, core)


def pair_partner_crossed(place):
    return other_core(pair_partner(place))


def other_core(place):
    return (*place[:4], 1 - place[4])


def other_half(place):
    xl, y, z, xh, core = place
    return (xl, y, z, 1 - xh, core)


def hop(stage, r):
    return (r + (JUMPS[stage] if r % 2 == 0 else -JUMPS[stage])) % Z


def ring_partner(stage):
    def partner(place):
        xl, y, z, xh, core = place
        z = hop(stage, z) if core == 0 else -hop(stage, -z % Z) % Z
        return (xl, y, z, xh, core)

    return partner


def keep_bits(stage):
    side, todo = {}, []
    for r in range(Z):
        if r in side:
            continue
        side[r], todo = 0, [r]
        while todo:
            at = todo.pop()
            for later in range(stage, len(JUMPS)):
                to, value = hop(later, at), side[at] ^ (later == stage)
                if to not in side:
                    side[to] = value
                    todo.append(to)
                assert side[to] == value
    return sum(side[r] << r for r in range(Z))


def fetch(value, source_of):
    return lax.ppermute(value, ("occ", "aux"), [(flat(source_of(p)), flat(p)) for p in places()])


def deliver(value, target_of):
    return lax.ppermute(value, ("occ", "aux"), [(flat(p), flat(target_of(p))) for p in places()])


def dot(left, right, dims):
    return lax.dot_general(left, right, (dims, ((), ())), precision=lax.Precision.HIGH, preferred_element_type=jnp.float32)


def table_pick(table, indices):
    matches = indices[:, None] == jnp.arange(table.shape[0], dtype=jnp.int32)[None, :]
    return jnp.sum(jnp.where(matches, table[None, :], 0.0), axis=1)


def scalar_pick(values, position):
    matches = jnp.arange(values.shape[0], dtype=jnp.int32) == position
    return jnp.sum(jnp.where(matches, values, jnp.zeros_like(values)))


def halves(value):
    half = value.shape[0] // 2
    return value[:half], value[half:]


def scattered(parts, upper, partner):
    halved = [halves(v) for v in parts]
    sent = [jnp.where(upper, low, high) for low, high in halved]
    kept = [jnp.where(upper, high, low) for low, high in halved]
    received = fetch(jnp.concatenate(sent, axis=1), partner)
    return jnp.concatenate(kept, axis=1) + received


def joined(value, received, upper):
    return jnp.concatenate([jnp.where(upper, received, value), jnp.where(upper, value, received)], axis=0)


def gathered(value, upper, partner):
    return joined(value, fetch(value, partner), upper)


def body(factors, occ_energy, vir_energy, orbital, vir_index):
    mine = factors[0]
    edges = [sum(SPLITS[:k]) for k in range(len(SPLITS) + 1)]
    spans = list(zip(edges, edges[1:]))
    near = fetch(mine, pair_partner)
    far = [fetch(mine[lo:hi], pair_partner_crossed) for lo, hi in spans]
    theirs = [[near[lo:hi], f] for (lo, hi), f in zip(spans, far)]
    own = [mine, fetch(mine, other_core)]

    occ, aux = lax.axis_index("occ"), lax.axis_index("aux")
    core, xh, z = aux & 1, (aux >> 1) & 1, aux >> 2
    xl, y = occ >> 2, occ & 3
    partner = jnp.where(core == 0, xl * Y + ((y + 1) & 3), (1 - xl) * Y + ((y + 3) & 3))
    ring = jnp.where(core == 0, z, -z & 15)
    keeps = [(jnp.int32(keep_bits(s)) >> ring) & 1 for s in range(3)]
    large = [(keeps[0] == 1, ring_partner(0)), (xh == 1, other_half)]
    small = [(keeps[1] == 1, ring_partner(1)), (keeps[2] == 1, ring_partner(2))]
    start = keeps[0] * 320 + xh * 160 + keeps[1] * 80 + keeps[2] * 40
    rows = 40

    virtual = table_pick(vir_energy, vir_index)
    virtual_rows = table_pick(vir_energy, lax.dynamic_slice(vir_index, (start,), (rows,)))
    energy = table_pick(occ_energy, orbital)
    pair_energy = scalar_pick(energy, occ) + scalar_pick(energy, partner)
    denominator = pair_energy - virtual_rows[:, None] - virtual[None, :]

    kept = [sum(dot(o, t, ((1,), (1,))) for o, t in zip(own, ts)) for ts in theirs]
    for upper, partner_of in large:
        kept = [scattered([k], upper, partner_of) for k in kept]
    for upper, partner_of in small:
        kept = [scattered(kept, upper, partner_of)]
    kept = kept[0] + fetch(kept[0], ring_partner(3))
    kept = kept / denominator
    for upper, partner_of in small[::-1]:
        kept = gathered(kept, upper, partner_of)
    kept = [kept[:, lo:hi] for lo, hi in spans]
    kept = [gathered(k, xh == 1, other_half) for k in kept]
    arrived = [fetch(k, ring_partner(0)) for k in kept]
    full, back = [], []
    for k, a in zip(kept, arrived):
        full.append(joined(k, a, keeps[0] == 1))
        terms = [dot(full[-1], o, ((0,), (0,))) for o in own[::-1]]
        pair = []
        for t, target in zip(terms, (pair_partner_crossed, pair_partner)):
            pair.append(deliver(t, target))
        back.append(pair)
    crossed = sum(dot(k, ts[1], ((1,), (0,))) for k, ts in zip(full, theirs))
    handed = fetch(crossed, other_core)
    straight = sum(dot(k, ts[0], ((1,), (0,))) for k, ts in zip(full, theirs))
    total = straight + handed
    returned = jnp.concatenate([a + b for a, b in back], axis=0)
    return (total + returned)[None]


def solution(mesh):
    return jax.shard_map(
        body,
        mesh=mesh,
        in_specs=(P("occ", None, "aux"), P(), P(), P(), P()),
        out_specs=P("occ", None, "aux"),
        check_vma=False,
    )
```

```python
import jax
import jax.numpy as jnp
from jax import lax
from jax.sharding import PartitionSpec as P


XL, Y, Z, XH, CORE = 2, 4, 16, 2, 2
SPLITS = (256, 384)
BACKWARD = (0, 1)
JUMPS = (1, -1, 3, -5)


def flat(place):
    xl, y, z, xh, core = place
    return (((xl * Y + y) * Z + z) * XH + xh) * CORE + core


def places():
    return [
        (xl, y, z, xh, core)
        for xl in range(XL)
        for y in range(Y)
        for z in range(Z)
        for xh in range(XH)
        for core in range(CORE)
    ]


def pair_partner(place):
    xl, y, z, xh, core = place
    return (xl, (y + 1) % Y, z, xh, core) if core == 0 else (1 - xl, (y - 1) % Y, z, xh, core)


def pair_partner_crossed(place):
    return other_core(pair_partner(place))


def other_core(place):
    return (*place[:4], 1 - place[4])


def other_half(place):
    xl, y, z, xh, core = place
    return (xl, y, z, 1 - xh, core)


def hop(stage, r):
    return (r + (JUMPS[stage] if r % 2 == 0 else -JUMPS[stage])) % Z


def ring_partner(stage):
    def partner(place):
        xl, y, z, xh, core = place
        z = hop(stage, z) if core == 0 else -hop(stage, -z % Z) % Z
        return (xl, y, z, xh, core)

    return partner


def keep_bits(stage):
    side, todo = {}, []
    for r in range(Z):
        if r in side:
            continue
        side[r], todo = 0, [r]
        while todo:
            at = todo.pop()
            for later in range(stage, len(JUMPS)):
                to, value = hop(later, at), side[at] ^ (later == stage)
                if to not in side:
                    side[to] = value
                    todo.append(to)
                assert side[to] == value
    return sum(side[r] << r for r in range(Z))


def fetch(value, source_of):
    return lax.ppermute(value, ("occ", "aux"), [(flat(source_of(p)), flat(p)) for p in places()])


def deliver(value, target_of):
    return lax.ppermute(value, ("occ", "aux"), [(flat(p), flat(target_of(p))) for p in places()])


def dot(left, right, dims):
    return lax.dot_general(left, right, (dims, ((), ())), precision=lax.Precision.HIGH, preferred_element_type=jnp.float32)


def table_pick(table, indices):
    matches = indices[:, None] == jnp.arange(table.shape[0], dtype=jnp.int32)[None, :]
    return jnp.sum(jnp.where(matches, table[None, :], 0.0), axis=1)


def scalar_pick(values, position):
    matches = jnp.arange(values.shape[0], dtype=jnp.int32) == position
    return jnp.sum(jnp.where(matches, values, jnp.zeros_like(values)))


def halves(value):
    half = value.shape[0] // 2
    return value[:half], value[half:]


def scattered(parts, upper, partner):
    halved = [halves(v) for v in parts]
    sent = [jnp.where(upper, low, high) for low, high in halved]
    kept = [jnp.where(upper, high, low) for low, high in halved]
    received = fetch(jnp.concatenate(sent, axis=1), partner)
    return jnp.concatenate(kept, axis=1) + received


def joined(value, received, upper):
    return jnp.concatenate([jnp.where(upper, received, value), jnp.where(upper, value, received)], axis=0)


def gathered(value, upper, partner):
    return joined(value, fetch(value, partner), upper)


def body(factors, occ_energy, vir_energy, orbital, vir_index):
    mine = factors[0]
    edges = [sum(SPLITS[:k]) for k in range(len(SPLITS) + 1)]
    spans = list(zip(edges, edges[1:]))
    near = fetch(mine, pair_partner)
    theirs = []
    for lo, hi in spans:
        theirs.append([near[lo:hi], fetch(mine[lo:hi], pair_partner_crossed)])
    own = [mine, fetch(mine, other_core)]

    occ, aux = lax.axis_index("occ"), lax.axis_index("aux")
    core, xh, z = aux & 1, (aux >> 1) & 1, aux >> 2
    xl, y = occ >> 2, occ & 3
    partner = jnp.where(core == 0, xl * Y + ((y + 1) & 3), (1 - xl) * Y + ((y + 3) & 3))
    ring = jnp.where(core == 0, z, -z & 15)
    keeps = [(jnp.int32(keep_bits(s)) >> ring) & 1 for s in range(2)]
    left, right = xh == 1, keeps[1] == 1
    start = keeps[0] * 320 + xh * 160 + keeps[1] * 80
    rows = 80

    virtual = table_pick(vir_energy, vir_index)
    virtual_rows = table_pick(vir_energy, lax.dynamic_slice(vir_index, (start,), (rows,)))
    energy = table_pick(occ_energy, orbital)
    pair_energy = scalar_pick(energy, occ) + scalar_pick(energy, partner)
    denominator = pair_energy - virtual_rows[:, None] - virtual[None, :]

    first = keeps[0] == 1
    own_kept, own_sent = [], []
    for o in own:
        low, high = halves(o)
        own_kept.append(jnp.where(first, high, low))
        own_sent.append(jnp.where(first, low, high))
    kept = []
    for ts in theirs:
        sent = sum(dot(o, t, ((1,), (1,))) for o, t in zip(own_sent, ts))
        received = fetch(sent, ring_partner(0))
        stay = lax.optimization_barrier(sum(dot(o, t, ((1,), (1,))) for o, t in zip(own_kept, ts)))
        kept.append(stay + received)
    for n, k in enumerate(kept):
        kept[n] = scattered([k], left, other_half)
    kept = [scattered(kept, right, ring_partner(1))]
    kept = kept[0]
    for stage in (2, 3):
        kept = kept + fetch(kept, ring_partner(stage))
    kept = kept / denominator
    kept = gathered(kept, right, ring_partner(1))
    full, back = [None] * len(spans), [None] * len(spans)
    kept = [kept[:, lo:hi] for lo, hi in spans]
    for n in BACKWARD:
        kept[n] = gathered(kept[n], left, other_half)
    for n in BACKWARD:
        received = fetch(kept[n], ring_partner(0))
        full[n] = joined(kept[n], received, first)
        early = lax.optimization_barrier([dot(kept[n], o, ((0,), (0,))) for o in own_kept[::-1]])
        terms = [e + dot(received, o, ((0,), (0,))) for e, o in zip(early, own_sent[::-1])]
        back[n] = []
        for t, target in zip(terms, (pair_partner_crossed, pair_partner)):
            back[n].append(deliver(t, target))
    crossed = sum(dot(k, ts[1], ((1,), (0,))) for k, ts in zip(full, theirs))
    handed = fetch(crossed, other_core)
    straight = lax.optimization_barrier(sum(dot(k, ts[0], ((1,), (0,))) for k, ts in zip(full, theirs)))
    total = straight + handed
    returned = jnp.concatenate([a + b for a, b in back], axis=0)
    return (total + returned)[None]


def solution(mesh):
    return jax.shard_map(
        body,
        mesh=mesh,
        in_specs=(P("occ", None, "aux"), P(), P(), P(), P()),
        out_specs=P("occ", None, "aux"),
        check_vma=False,
    )
```
